32 devices in a mesh: dp: 32 (over z, y, x, core).
Axes of the slice: x: 2, y: 2, z: 4, core: 2. Of those that a mesh axis runs over, the one named last changes fastest.
Arguments:
- images: bfloat16 [64, 197, 384], P('dp'), may hold values from -6 to 6
- params: bfloat16 [1, 1777664], P(None, 'dp'), as said below
- counts: int32 [32], P('dp'), may hold values from 1 to 2, as said below
- grad_out: bfloat16 [64, 197, 384], P('dp'), may hold values from -6 to 6
Outputs:
- activations: bfloat16 [64, 197, 384], P('dp')
- grad_input: float32 [64, 197, 384], P('dp')
- grad_params: float32 [1, 1777664], P(None, 'dp')
The draws below stay inside these ranges and needn't reach their ends.
Inputs may be any that keep to these rules, and one draw needn't show every extreme that they name: `counts`: the live images of each device; some device holds 2 and some device holds 1. `params`: laid out as the steps say; gains lie between 0.5 and 1.5.
All inputs are finite; a program needn't handle non-finite values.
Results may differ from the reference program's by a relative error of at most 0.011.
Values may be sent and summed in bfloat16 or wider, within the bound.
No kernel may reach another device: no remote copies, remote signals or barrier semaphores. Data moves between devices by JAX's collectives and lax.ppermute only.
A program may use at most 64 MiB of HBM per device.

```python
import math
import jax
import jax.numpy as jnp
import numpy as np
from jax import lax

D = 384
HEADS = 6
HEAD_DIM = 64
FF = 1536
S = 197
LAYERS = 1
SLOTS = 2
SHARDS = 32
IMAGES = 64
PARAMS = 1774080
FLAT = 1777664


def draw_params(key, part):
    three = 3 * D
    segments = [(D, 'gain', 0.0), (D, 'bias', 0.5), (D * three, 'qkv', D ** (-0.5)), (D, 'bias', 0.5), (D, 'bias', 0.5), (D * D, 'out', 6.0 * D ** (-0.5)), (D, 'bias', 0.5), (D, 'gain', 0.0), (D, 'bias', 0.5), (D * FF, 'up', D ** (-0.5)), (FF, 'bias', 0.5), (FF * D, 'down', 1.5 * FF ** (-0.5)), (D, 'bias', 0.5)]
    factor = np.ones((FLAT,), np.float32)
    gainflag = np.zeros((FLAT,), np.float32)
    qmark = np.zeros((FLAT,), np.bool_)
    kmark = np.zeros((FLAT,), np.bool_)
    offset = 0
    for number, label, coeff in segments:
        if label == 'gain':
            factor[offset:offset + number] = 0.0
            gainflag[offset:offset + number] = 1.0
        else:
            factor[offset:offset + number] = coeff
        if label == 'qkv':
            rows = np.arange(D)[:, None] * three + offset
            cols = np.arange(HEAD_DIM)[None, :]
            qmark[(rows + cols).reshape(-1)] = True
            kmark[(rows + cols + D).reshape(-1)] = True
        offset = offset + number
    first, second = jax.random.split(key)
    spread = jax.random.uniform(second, (LAYERS, FLAT), jnp.float32)
    base = jax.random.truncated_normal(first, -4.0, 4.0, (LAYERS, FLAT), jnp.float32)
    values = jnp.asarray(factor) * base + jnp.asarray(gainflag) * (0.5 + spread)
    return values.astype(jnp.bfloat16)


def draw_counts(key, part):
    first, second, third = jax.random.split(key, 3)
    drawn = jax.random.randint(first, (SHARDS,), 1, SLOTS + 1)
    top = jax.random.randint(second, (), 0, SHARDS)
    other = (top + 1 + jax.random.randint(third, (), 0, SHARDS - 1)) % SHARDS
    drawn = drawn.at[top].set(SLOTS).at[other].set(1)
    return drawn.astype(jnp.int32)


def block_scale(own_key, dims, cuts, smallest, largest):
    loudness = 1.0
    for axis_at, blocks in cuts:
        draws = jax.random.uniform(jax.random.fold_in(jax.random.fold_in(own_key, 6), axis_at), (blocks,), jnp.float32, smallest / len(cuts), largest / len(cuts))
        loudness = loudness * jnp.repeat(jnp.exp(draws), dims[axis_at] // blocks).reshape((-1,) + (1,) * (len(dims) - 1 - axis_at))
    return loudness


def bell_draw(own_key, dims, scale, limit, cuts=(), held_as=jnp.bfloat16):
    entries = jax.random.normal(own_key, dims, jnp.float32) * scale
    if len(cuts) > 0:
        entries = block_scale(own_key, dims, cuts, -0.22, 0.18) * entries
    return jnp.clip(entries, min=-limit, max=limit).astype(held_as)


def setup_inputs(seed: int = 0) -> dict:
    key_list = jax.random.split(jax.random.key(seed), 5)
    return {
        "images": bell_draw(key_list[0], (IMAGES, S, D), 1.0, 6.0, ((0, 32),)),
        "params": draw_params(jax.random.fold_in(key_list[4], 71), 0),
        "counts": draw_counts(jax.random.fold_in(key_list[4], 71), 0),
        "grad_out": bell_draw(key_list[3], (IMAGES, S, D), 1.0, 6.0, ((0, 32),)),
    }


EPS = 1e-06

def batch_mm(form, left, right):
    return jnp.einsum(form, left.astype(jnp.float32), right.astype(jnp.float32))

def flat_dot(left, right):
    batch, length, inner = left.shape
    return jnp.dot(left.reshape(batch * length, inner), right, preferred_element_type=jnp.float32).reshape(batch, length, right.shape[1])

def back_dot(left, right):
    batch, length, inner = left.shape
    product = lax.dot_general(left.reshape(batch * length, inner), right, (((1,), (1,)), ((), ())), preferred_element_type=jnp.float32)
    return product.reshape(batch, length, right.shape[0])

def weight_grad(left, right):
    return lax.dot_general(left.reshape(-1, left.shape[2]), right.reshape(-1, right.shape[2]), (((0,), (0,)), ((), ())), preferred_element_type=jnp.float32)

def gelu_slope(values):
    return 0.5 * (1.0 + lax.erf(values * 0.7071067811865476)) + values * jnp.exp(-0.5 * values * values) * 0.3989422804014327

def layer_shapes(width, hidden):
    return [(width,), (width,), (width, 3 * width), (width,), (width,), (width, width), (width,), (width,), (width,), (width, hidden), (hidden,), (hidden, width), (width,)]

def unpack(flat, width, hidden):
    parts = []
    offset = 0
    for shape in layer_shapes(width, hidden):
        number = math.prod(shape)
        parts.append(flat[offset:offset + number].reshape(shape))
        offset = offset + number
    return parts

def pack(grads, target):
    flat = jnp.concatenate([item.reshape(-1) for item in grads])
    return jnp.pad(flat, (0, target - flat.shape[0]))

def layer_norm(stream, gain, bias):
    mean = lax.optimization_barrier(jnp.mean(stream, axis=-1, keepdims=True))
    centred = stream - mean
    variance = lax.optimization_barrier(jnp.mean(centred * centred, axis=-1, keepdims=True))
    inv_std = lax.rsqrt(variance + EPS)
    normed = centred * inv_std
    return (normed * gain + bias, normed, inv_std)

def norm_back(grad, normed, inv_std, gain):
    grad_gain = lax.optimization_barrier(jnp.sum(grad * normed, axis=(0, 1)))
    grad_bias = lax.optimization_barrier(jnp.sum(grad, axis=(0, 1)))
    scaled = grad * gain
    grad_in = inv_std * (scaled - lax.optimization_barrier(jnp.mean(scaled, axis=-1, keepdims=True)) - normed * lax.optimization_barrier(jnp.mean(scaled * normed, axis=-1, keepdims=True)))
    return (grad_in, grad_gain, grad_bias)

def forward_layer(parts, stream, heads):
    gain_one, bias_one, w_qkv, q_bias, v_bias, w_out, out_bias, gain_two, bias_two, w_up, up_bias, w_down, down_bias = parts
    batch, length, width = stream.shape
    head_dim = width // heads
    scale = head_dim ** (-0.5)
    shifted, normed_one, inv_one = layer_norm(stream, gain_one.astype(jnp.float32), bias_one.astype(jnp.float32))
    input_one = shifted.astype(jnp.bfloat16)
    qkv_bias = jnp.concatenate([q_bias.astype(jnp.float32), jnp.zeros((width,), jnp.float32), v_bias.astype(jnp.float32)])
    project = flat_dot(input_one, w_qkv) + qkv_bias
    split = project.reshape(batch, length, 3, heads, head_dim).astype(jnp.bfloat16)
    queries, keys, values = (split[:, :, 0], split[:, :, 1], split[:, :, 2])
    scores = batch_mm('bqhe,bkhe->bhqk', queries, keys) * scale
    peak = lax.optimization_barrier(jnp.max(scores, axis=-1, keepdims=True))
    logsum = peak[..., 0] + jnp.log(lax.optimization_barrier(jnp.sum(jnp.exp(scores - peak), axis=-1)))
    weights = jnp.exp(scores - logsum[..., None]).astype(jnp.bfloat16)
    mixed = batch_mm('bhqk,bkhe->bqhe', weights, values).astype(jnp.bfloat16)
    middle = stream + flat_dot(mixed.reshape(batch, length, width), w_out) + out_bias.astype(jnp.float32)
    shifted_two, normed_two, inv_two = layer_norm(middle, gain_two.astype(jnp.float32), bias_two.astype(jnp.float32))
    input_two = shifted_two.astype(jnp.bfloat16)
    pre_act = flat_dot(input_two, w_up) + up_bias.astype(jnp.float32)
    hidden = jax.nn.gelu(pre_act, approximate=False).astype(jnp.bfloat16)
    result = middle + flat_dot(hidden, w_down) + down_bias.astype(jnp.float32)
    cache = (normed_one, inv_one, input_one, queries, keys, values, logsum, mixed, normed_two, inv_two, input_two, pre_act, hidden)
    return (result, cache)

def backward_layer(parts, cache, grad_result, heads):
    gain_one, bias_one, w_qkv, q_bias, v_bias, w_out, out_bias, gain_two, bias_two, w_up, up_bias, w_down, down_bias = parts
    normed_one, inv_one, input_one, queries, keys, values, logsum, mixed, normed_two, inv_two, input_two, pre_act, hidden = cache
    batch, length, width = grad_result.shape
    head_dim = width // heads
    scale = head_dim ** (-0.5)
    grad_low = grad_result.astype(jnp.bfloat16)
    grad_down = weight_grad(hidden, grad_low)
    grad_down_bias = lax.optimization_barrier(jnp.sum(grad_result, axis=(0, 1)))
    grad_pre = back_dot(grad_low, w_down) * gelu_slope(pre_act)
    pre_low = grad_pre.astype(jnp.bfloat16)
    grad_up = weight_grad(input_two, pre_low)
    grad_up_bias = lax.optimization_barrier(jnp.sum(grad_pre, axis=(0, 1)))
    grad_input_two = back_dot(pre_low, w_up)
    norm_grad_two, grad_gain_two, grad_bias_two = norm_back(grad_input_two, normed_two, inv_two, gain_two.astype(jnp.float32))
    grad_middle = grad_result + norm_grad_two
    middle_low = grad_middle.astype(jnp.bfloat16)
    mixed_flat = mixed.reshape(batch, length, width)
    grad_out_w = weight_grad(mixed_flat, middle_low)
    grad_out_bias = lax.optimization_barrier(jnp.sum(grad_middle, axis=(0, 1)))
    grad_mixed = back_dot(middle_low, w_out).astype(jnp.bfloat16).reshape(batch, length, heads, head_dim)
    scores = batch_mm('bqhe,bkhe->bhqk', queries, keys) * scale
    probs = jnp.exp(scores - logsum[..., None])
    weights = probs.astype(jnp.bfloat16)
    grad_values = batch_mm('bhqk,bqhe->bkhe', weights, grad_mixed)
    grad_weights = batch_mm('bqhe,bkhe->bhqk', grad_mixed, values)
    row_dot = jnp.einsum('bqhe,bqhe->bhq', grad_mixed.astype(jnp.float32), mixed.astype(jnp.float32))
    grad_scores = (probs * (grad_weights - row_dot[..., None]) * scale).astype(jnp.bfloat16)
    grad_queries = batch_mm('bhqk,bkhe->bqhe', grad_scores, keys)
    grad_keys = batch_mm('bhqk,bqhe->bkhe', grad_scores, queries)
    grad_q_bias = lax.optimization_barrier(jnp.sum(grad_queries, axis=(0, 1))).reshape(width)
    grad_v_bias = lax.optimization_barrier(jnp.sum(grad_values, axis=(0, 1))).reshape(width)
    grad_project = jnp.stack([grad_queries, grad_keys, grad_values], axis=2).reshape(batch, length, 3 * width).astype(jnp.bfloat16)
    grad_qkv = weight_grad(input_one, grad_project)
    grad_input_one = back_dot(grad_project, w_qkv)
    norm_grad_one, grad_gain_one, grad_bias_one = norm_back(grad_input_one, normed_one, inv_one, gain_one.astype(jnp.float32))
    grad_stream = grad_middle + norm_grad_one
    grads = (grad_gain_one, grad_bias_one, grad_qkv, grad_q_bias, grad_v_bias, grad_out_w, grad_out_bias, grad_gain_two, grad_bias_two, grad_up, grad_up_bias, grad_down, grad_down_bias)
    return (grad_stream, grads)

def reference(images, params, counts, grad_out):
    total = jnp.sum(counts).astype(jnp.float32)
    length_flat = params.shape[1]
    layers = [unpack(params[index], D, FF) for index in range(LAYERS)]
    blocks_in = images.reshape(SHARDS, SLOTS, S, D)
    blocks_grad = grad_out.reshape(SHARDS, SLOTS, S, D)

    def one_block(carry, inputs):
        block_in, block_grad, count = inputs
        live = (jnp.arange(SLOTS) < count).astype(jnp.float32)[:, None, None]
        stream = block_in.astype(jnp.float32)
        caches = []
        for index in range(LAYERS):
            stream, cache = forward_layer(layers[index], stream, HEADS)
            caches.append(cache)
        output = stream.astype(jnp.bfloat16) * live.astype(jnp.bfloat16)
        grad_stream = block_grad.astype(jnp.float32) * live
        new_carry = list(carry)
        for index in reversed(range(LAYERS)):
            grad_stream, grads = backward_layer(layers[index], caches[index], grad_stream, HEADS)
            new_carry[index] = carry[index] + pack(grads, PARAMS)
        return (tuple(new_carry), (output, grad_stream))
    start = tuple((jnp.zeros((PARAMS,), jnp.float32) for index in range(LAYERS)))
    sums, (outputs, grads_in) = lax.scan(one_block, start, (blocks_in, blocks_grad, counts))
    grad_params = jnp.stack([jnp.pad(item / total, (0, length_flat - PARAMS)) for item in sums])
    return (outputs.reshape(IMAGES, S, D), grads_in.reshape(IMAGES, S, D), grad_params)
```

```python
import functools

import jax
import jax.numpy as jnp
from jax import lax
from jax.experimental import pallas as pl
from jax.experimental.pallas import tpu as pltpu
from jax.sharding import PartitionSpec as P

HEADS = 6
FF = 1536
EPS = 1e-06
LANES = 128
F32 = jnp.float32
BF16 = jnp.bfloat16
VMEM_LIMIT = 60 * 1024 * 1024


class Plan:
    def __init__(self, n, width, hidden, flat, length):
        self.n = n
        self.width, self.hidden = width, hidden
        self.w, self.f = width // LANES, hidden // LANES
        self.length = length
        self.tokens = -(-length // 16) * 16
        self.shard = flat // n // LANES
        self.groups = n // 8
        self.early = self.groups // 4
        self.late = self.groups - self.early
        w, f = self.w, self.f
        sizes = [
            ("gain_one", w),
            ("bias_one", w),
            ("w_qkv", width * 3 * w),
            ("q_bias", w),
            ("v_bias", w),
            ("w_out", width * w),
            ("out_bias", w),
            ("gain_two", w),
            ("bias_two", w),
            ("w_up", width * f),
            ("up_bias", f),
            ("w_down", hidden * w),
            ("down_bias", w),
        ]
        self.at = {}
        row = 0
        for name, count in sizes:
            self.at[name] = row
            row += count
        self.used = row
        self.rows = flat // LANES
        self.split = self.early * 8 * self.shard
        self.base = self.at["w_out"] // 8 * 8
        self.tail = self.split - self.base
        assert self.base <= self.at["w_out"] <= self.split


def lane_mask(rows):
    return lax.broadcasted_iota(jnp.int32, (rows, LANES), 1) < LANES // 2


def load_vec(ref, row, count):
    return jnp.concatenate([ref[row + i : row + i + 1, :] for i in range(count)], axis=1)


def load_mat(ref, row, rows, count, out):
    for c in range(count):
        out[:, c * LANES : (c + 1) * LANES] = ref[pl.ds(row + c, rows, stride=count), :].astype(BF16)


def store_vec(ref, row, count, value):
    for i in range(count):
        ref[row + i : row + i + 1, :] = value[:, i * LANES : (i + 1) * LANES]


def store_mat(ref, row, rows, count, value, first=0):
    for c in range(value.shape[1] // LANES):
        ref[pl.ds(row + first + c, rows, stride=count), :] = value[:, c * LANES : (c + 1) * LANES]


def dot(left, right):
    return lax.dot_general(left, right, (((1,), (0,)), ((), ())), preferred_element_type=F32)


def dot_nt(left, right):
    return lax.dot_general(left, right, (((1,), (1,)), ((), ())), preferred_element_type=F32)


def dot_tn(left, right):
    return lax.dot_general(left, right, (((0,), (0,)), ((), ())), preferred_element_type=F32)


def norm(stream):
    mean = jnp.mean(stream, axis=-1, keepdims=True)
    centred = stream - mean
    variance = jnp.mean(centred * centred, axis=-1, keepdims=True)
    inv_std = lax.rsqrt(variance + EPS)
    return centred * inv_std, inv_std


def norm_back(grad, normed, inv_std, gain):
    grad_gain = jnp.sum(grad * normed, axis=0, keepdims=True)
    grad_bias = jnp.sum(grad, axis=0, keepdims=True)
    scaled = grad * gain
    grad_in = inv_std * (
        scaled
        - jnp.mean(scaled, axis=-1, keepdims=True)
        - normed * jnp.mean(scaled * normed, axis=-1, keepdims=True)
    )
    return grad_in, grad_gain, grad_bias


def axis_bits(core):
    return 2 + 2 * core, 4 - 2 * core


def piece_owner(me, piece):
    low = me % 8
    core = low % 2
    if piece & 4:
        low = low ^ 1
        core = 1 - core
    first, second = axis_bits(core)
    if piece & 1:
        low = low ^ first
    if piece & 2:
        low = low ^ second
    return low


def mixed_pairs(n, flip):
    return [(i, i ^ axis_bits(i % 2)[flip]) for i in range(n)]


def bit_pairs(n, bit):
    return [(i, i ^ bit) for i in range(n)]


def fetch(plan, pieces, landing, sems, me):
    copies = []
    for p, piece in enumerate(pieces):
        copies.append(
            pltpu.make_async_copy(piece, landing.at[piece_owner(me, p)], sems.at[p])
        )
    for copy in copies:
        copy.start()
    for copy in copies:
        copy.wait()


def unpack_rows(plan, landing, flat, first_group, groups, origin, cnt):
    for t in range(groups):
        for low in range(8):
            row = ((first_group + t) * 8 + low) * plan.shard - origin
            block = landing[low, t].astype(F32)
            flat[row : row + plan.shard, :] = block[: plan.shard]
            cnt = cnt + block[plan.shard : plan.shard + 1]
    return cnt


def pack_rows(plan, flat, first_group, groups, origin, keep, send, me):
    mine = me % 8
    for t in range(groups):
        for low in range(8):
            row = ((first_group + t) * 8 + low) * plan.shard - origin
            rel = mine ^ low
            pair = rel // 2
            swapped = (pair % 2) * 2 + pair // 2
            core = me % 2
            stays = rel % 2 == 0
            holder = jnp.where(stays, core, 1 - core)
            place = jnp.where(holder == 1, swapped, pair)

            @pl.when(stays)
            def _(row=row, place=place, t=t):
                keep[place, t] = flat[row : row + plan.shard, :]

            @pl.when(jnp.logical_not(stays))
            def _(row=row, place=place, t=t):
                send[place, t] = flat[row : row + plan.shard, :].astype(BF16)


def order_kernel(plan, rels, *refs):
    ins, (early, late) = refs[: len(rels)], refs[len(rels) :]
    mine = lax.axis_index("dp") // 8
    for block, group in zip(ins, rels):
        for i, rel in enumerate(group):
            t = mine ^ rel

            @pl.when(t < plan.early)
            def _(block=block, i=i, t=t):
                early[t] = block[i]

            @pl.when(t >= plan.early)
            def _(block=block, i=i, t=t):
                late[t - plan.early] = block[i]


def attend_kernel(plan, x_ref, *refs):
    pieces = refs[:8]
    in_one, qkv, mixed, lse, w_qkv, vecs, tail, cnt_ref = refs[8:16]
    landing, flat, sems = refs[16:]
    me = lax.axis_index("dp")
    at, w, width = plan.at, plan.w, plan.width
    tokens = plan.tokens
    fetch(plan, pieces, landing, sems, me)
    cnt_ref[...] = unpack_rows(plan, landing, flat, 0, plan.early, 0, jnp.zeros((1, LANES), F32))
    tail[...] = flat[plan.base : plan.split, :]
    load_mat(flat, at["w_qkv"], width, 3 * w, w_qkv)
    gain = load_vec(flat, at["gain_one"], w)
    bias = load_vec(flat, at["bias_one"], w)
    vecs[0:1, :] = gain
    normed, _ = norm(x_ref[...].astype(F32))
    shifted = (normed * gain + bias).astype(BF16)
    in_one[...] = shifted
    biases = [load_vec(flat, at["q_bias"], w), None, load_vec(flat, at["v_bias"], w)]
    for third in range(3):
        cols = slice(third * width, (third + 1) * width)
        project = dot(shifted, w_qkv[:, cols])
        if biases[third] is not None:
            project = project + biases[third]
        qkv[:, cols] = project.astype(BF16)
    scale = (width // HEADS) ** (-0.5)
    mask = lane_mask(tokens)
    valid = lax.broadcasted_iota(jnp.int32, (2 * tokens, tokens), 1) < plan.length
    zero = jnp.zeros((tokens, LANES), BF16)
    for b in range(x_ref.shape[0] // tokens):
        rows = slice(b * tokens, (b + 1) * tokens)
        for p in range(w):
            q = qkv[rows, p * LANES : (p + 1) * LANES]
            k = qkv[rows, width + p * LANES : width + (p + 1) * LANES]
            v = qkv[rows, 2 * width + p * LANES : 2 * width + (p + 1) * LANES]
            q2 = jnp.concatenate([jnp.where(mask, q, zero), jnp.where(mask, zero, q)], axis=0)
            scores = jnp.where(valid, dot_nt(q2, k) * scale, -1e30)
            peak = jnp.max(scores, axis=-1, keepdims=True)
            exps = jnp.exp(scores - peak)
            total = jnp.sum(exps, axis=-1, keepdims=True)
            lse[b * w + p] = peak + jnp.log(total)
            weights = (exps * (1.0 / total)).astype(BF16)
            out = dot(weights, v)
            mixed[rows, p * LANES : (p + 1) * LANES] = jnp.where(
                mask, out[:tokens], out[tokens:]
            ).astype(BF16)


def mlp_kernel(plan, chunk, counts, x_ref, grad_ref, mixed_ref, tail_ref, cnt_ref, *refs):
    pieces = refs[:8]
    act, grad_mid, grad_mixed, keep, send, tail, total = refs[8:15]
    landing, flat, w_out, w_up, w_down, acc, grad_in, sems = refs[15:]
    me = lax.axis_index("dp")
    at, w, f, width = plan.at, plan.w, plan.f, plan.width
    tokens, base = plan.tokens, plan.base
    slots = x_ref.shape[0] // tokens
    fetch(plan, pieces, landing, sems, me)
    flat[0 : plan.tail, :] = tail_ref[...]
    total[...] = unpack_rows(
        plan, landing, flat, plan.early, plan.late, base, cnt_ref[...]
    )
    load_mat(flat, at["w_out"] - base, width, w, w_out)
    load_mat(flat, at["w_up"] - base, width, f, w_up)
    load_mat(flat, at["w_down"] - base, plan.hidden, w, w_down)
    vec = lambda name, count: load_vec(flat, at[name] - base, count)
    out_bias, gain, bias = vec("out_bias", w), vec("gain_two", w), vec("bias_two", w)
    up_bias, down_bias = vec("up_bias", f), vec("down_bias", w)

    row = lax.broadcasted_iota(jnp.int32, (slots * tokens, 1), 0)
    live = (row < counts[0] * tokens).astype(F32)
    grad = grad_ref[...].astype(F32) * live
    grad_low = grad.astype(BF16)
    mixed = mixed_ref[...]
    middle = x_ref[...].astype(F32) + dot(mixed, w_out[...]) + out_bias
    normed, inv_std = norm(middle)
    in_two = (normed * gain + bias).astype(BF16)
    in_two_t = in_two.T
    store_vec(flat, at["down_bias"] - base, w, jnp.sum(grad, axis=0, keepdims=True))
    for c in range(plan.hidden // chunk):
        cols = slice(c * chunk, (c + 1) * chunk)
        pre = dot(in_two, w_up[:, cols]) + up_bias[:, cols]
        phi = 0.5 * (1.0 + lax.erf(pre * 0.7071067811865476))
        slope = phi + pre * jnp.exp(-0.5 * pre * pre) * 0.3989422804014327
        hidden = (pre * phi).astype(BF16)
        grad_pre = dot_nt(grad_low, w_down[cols, :]) * slope
        pre_low = grad_pre.astype(BF16)
        out = dot(hidden, w_down[cols, :])
        back = dot_nt(pre_low, w_up[:, cols])
        if c == 0:
            acc[...] = out
            grad_in[...] = back
        else:
            acc[...] += out
            grad_in[...] += back
        store_mat(
            flat, at["w_down"] - base + c * chunk * w, chunk, w, dot_tn(hidden, grad_low)
        )
        store_mat(
            flat, at["w_up"] - base, width, f, dot(in_two_t, pre_low), c * chunk // LANES
        )
        store_vec(
            flat,
            at["up_bias"] - base + c * chunk // LANES,
            chunk // LANES,
            jnp.sum(grad_pre, axis=0, keepdims=True),
        )
    result = ((middle + acc[...] + down_bias) * live).astype(BF16)
    for b in range(slots):
        act[b] = result[b * tokens : b * tokens + plan.length]
    norm_grad, grad_gain, grad_bias = norm_back(grad_in[...], normed, inv_std, gain)
    mid = grad + norm_grad
    grad_mid[...] = mid
    mid_low = mid.astype(BF16)
    store_vec(flat, at["gain_two"] - base, w, grad_gain)
    store_vec(flat, at["bias_two"] - base, w, grad_bias)
    store_vec(flat, at["out_bias"] - base, w, jnp.sum(mid, axis=0, keepdims=True))
    store_mat(flat, at["w_out"] - base, width, w, dot_tn(mixed, mid_low))
    grad_mixed[...] = dot_nt(mid_low, w_out[...]).astype(BF16)
    if plan.rows > plan.used:
        flat[plan.used - base :, :] = jnp.zeros((plan.rows - plan.used, LANES), F32)
    tail[...] = flat[0 : plan.tail, :]
    pack_rows(plan, flat, plan.early, plan.late, base, keep, send, me)


def back_kernel(
    plan, x_ref, in_one, qkv, mixed_ref, lse, w_qkv, vecs, grad_mid, grad_mixed, tail, *refs
):
    grad_input, keep, send = refs[:3]
    flat, proj = refs[3:]
    me = lax.axis_index("dp")
    at, w, width = plan.at, plan.w, plan.width
    tokens = plan.tokens
    slots = x_ref.shape[0] // tokens
    scale = (width // HEADS) ** (-0.5)
    mask = lane_mask(tokens)
    valid = lax.broadcasted_iota(jnp.int32, (2 * tokens, tokens), 1) < plan.length
    zero = jnp.zeros((tokens, LANES), BF16)
    flat[plan.base : plan.split, :] = tail[...]
    both = lambda v: jnp.concatenate([jnp.where(mask, v, zero), jnp.where(mask, zero, v)], axis=0)
    for p in range(w):
        cut = slice(p * LANES, (p + 1) * LANES)
        q_sum = jnp.zeros((1, LANES), F32)
        v_sum = jnp.zeros((1, LANES), F32)
        for b in range(slots):
            rows = slice(b * tokens, (b + 1) * tokens)
            q = qkv[rows, cut]
            k = qkv[rows, width + p * LANES : width + (p + 1) * LANES]
            v = qkv[rows, 2 * width + p * LANES : 2 * width + (p + 1) * LANES]
            q2 = both(q)
            g2 = both(grad_mixed[rows, cut])
            m = mixed_ref[rows, cut].astype(F32)
            scores = dot_nt(q2, k) * scale
            probs = jnp.where(valid, jnp.exp(scores - lse[b * w + p]), 0.0)
            weights = probs.astype(BF16)
            grad_values = dot_tn(weights, g2)
            grad_weights = dot_nt(g2, v)
            row_dot = jnp.sum(
                g2.astype(F32) * jnp.concatenate([m, m], axis=0), axis=-1, keepdims=True
            )
            grad_scores = (probs * (grad_weights - row_dot) * scale).astype(BF16)
            pair = dot(grad_scores, k)
            grad_queries = jnp.where(mask, pair[:tokens], pair[tokens:])
            grad_keys = dot_tn(grad_scores, q2)
            q_sum = q_sum + jnp.sum(grad_queries, axis=0, keepdims=True)
            v_sum = v_sum + jnp.sum(grad_values, axis=0, keepdims=True)
            proj[rows, cut] = grad_queries.astype(BF16)
            proj[rows, width + p * LANES : width + (p + 1) * LANES] = grad_keys.astype(BF16)
            proj[rows, 2 * width + p * LANES : 2 * width + (p + 1) * LANES] = grad_values.astype(
                BF16
            )
        flat[at["q_bias"] + p : at["q_bias"] + p + 1, :] = q_sum
        flat[at["v_bias"] + p : at["v_bias"] + p + 1, :] = v_sum
    in_one_t = in_one[...].T
    for third in range(3):
        cols = slice(third * width, (third + 1) * width)
        store_mat(
            flat, at["w_qkv"], width, 3 * w, dot(in_one_t, proj[:, cols]), third * w
        )
    grad_in = dot_nt(proj[...], w_qkv[...])
    normed, inv_std = norm(x_ref[...].astype(F32))
    norm_grad, grad_gain, grad_bias = norm_back(grad_in, normed, inv_std, vecs[0:1, :])
    store_vec(flat, at["gain_one"], w, grad_gain)
    store_vec(flat, at["bias_one"], w, grad_bias)
    result = grad_mid[...] + norm_grad
    for b in range(slots):
        grad_input[b] = result[b * tokens : b * tokens + plan.length]
    pack_rows(plan, flat, 0, plan.early, 0, keep, send, me)


def join_kernel(plan, early, early_in, late, late_in, keep, send):
    mine = lax.axis_index("dp") // 8
    for t in range(plan.groups):
        if t < plan.early:
            kept, came = early.at[0, t], early_in.at[t]
        else:
            kept, came = late.at[0, t - plan.early], late_in.at[t - plan.early]
        rel = mine ^ t

        @pl.when(rel % 2 == 0)
        def _(kept=kept, came=came, rel=rel):
            keep[rel // 2] = kept[...] + came[...].astype(F32)

        @pl.when(rel % 2 == 1)
        def _(kept=kept, came=came, rel=rel):
            send[rel // 2] = (kept[...] + came[...].astype(F32)).astype(BF16)


def vmem():
    return pl.BlockSpec(memory_space=pltpu.VMEM)


def hbm():
    return pl.BlockSpec(memory_space=pl.ANY)


def call(kernel, ins, specs, outs, scratch=(), name=None, flops=0, moved=0):
    return pl.pallas_call(
        kernel,
        in_specs=specs,
        out_specs=tuple(vmem() for _ in outs),
        out_shape=tuple(jax.ShapeDtypeStruct(s, d) for s, d in outs),
        scratch_shapes=list(scratch),
        compiler_params=pltpu.CompilerParams(vmem_limit_bytes=VMEM_LIMIT),
        cost_estimate=pl.CostEstimate(flops=flops, bytes_accessed=moved, transcendentals=0),
        name=name,
    )(*ins)


def gather(plan, block):
    n = plan.n
    parts = [(block, [0])]
    bit = n // 2
    while bit >= 8:
        sent = parts[0] if len(parts) == 1 else (
            jnp.concatenate([a for a, _ in parts], axis=0),
            [r for _, g in parts for r in g],
        )
        came = lax.ppermute(sent[0], "dp", bit_pairs(n, bit))
        parts = parts + [(came, [r ^ (bit // 8) for r in sent[1]])]
        bit //= 2
    rows = block.shape[1:]
    early, late = call(
        functools.partial(order_kernel, plan, [g for _, g in parts]),
        [a for a, _ in parts],
        [vmem()] * len(parts),
        [((plan.early,) + rows, BF16), ((plan.late,) + rows, BF16)],
        name="order",
    )

    def plane(own):
        pieces = [own]
        for flip in (0, 1):
            pieces = pieces + [lax.ppermute(p, "dp", mixed_pairs(n, flip)) for p in pieces]
        return pieces + [lax.ppermute(p, "dp", bit_pairs(n, 1)) for p in pieces]

    return plane(early), plane(late)


def plane_sum(plan, keep, send):
    n = plan.n
    acc = keep + lax.ppermute(send, "dp", bit_pairs(n, 1)).astype(F32)
    came = lax.ppermute(acc[2:].astype(BF16), "dp", mixed_pairs(n, 1))
    acc = acc[:2] + came.astype(F32)
    came = lax.ppermute(acc[1].astype(BF16), "dp", mixed_pairs(n, 0))
    return acc, came


def body(plan, images, params, counts, grad_out):
    slots, length, width = images.shape
    n, tokens = plan.n, plan.tokens
    count_row = jnp.broadcast_to(counts.astype(BF16)[:, None, None], (1, 1, LANES))
    block = jnp.concatenate([params.reshape(1, plan.shard, LANES), count_row], axis=1)
    early, late = gather(plan, block)

    pad = ((0, 0), (0, tokens - length), (0, 0))
    x = jnp.pad(images, pad).reshape(slots * tokens, width)
    grad = jnp.pad(grad_out, pad).reshape(slots * tokens, width)
    m = slots * tokens
    w, f, hidden = plan.w, plan.f, plan.hidden
    block_rows = plan.shard + 1
    late_rows = plan.rows - plan.base

    in_one, qkv, mixed, lse, w_qkv, vecs, tail, cnt = call(
        functools.partial(attend_kernel, plan),
        [x] + early,
        [vmem()] + [hbm()] * 8,
        [
            ((m, width), BF16),
            ((m, 3 * width), BF16),
            ((m, width), BF16),
            ((slots * w, 2 * tokens, 1), F32),
            ((width, 3 * width), BF16),
            ((8, width), F32),
            ((plan.tail, LANES), F32),
            ((1, LANES), F32),
        ],
        [
            pltpu.VMEM((8, plan.early, block_rows, LANES), BF16),
            pltpu.VMEM((plan.split, LANES), F32),
            pltpu.SemaphoreType.DMA((8,)),
        ],
        name="attend",
        flops=2 * m * width * 3 * width,
        moved=4 * plan.split * LANES,
    )
    act, grad_mid, grad_mixed, keep_late, send_late, tail, total = call(
        functools.partial(mlp_kernel, plan, 2 * LANES),
        [counts, x, grad, mixed, tail, cnt] + late,
        [pl.BlockSpec(memory_space=pltpu.SMEM)] + [vmem()] * 5 + [hbm()] * 8,
        [
            ((slots, length, width), BF16),
            ((m, width), F32),
            ((m, width), BF16),
            ((4, plan.late, plan.shard, LANES), F32),
            ((4, plan.late, plan.shard, LANES), BF16),
            ((plan.tail, LANES), F32),
            ((1, LANES), F32),
        ],
        [
            pltpu.VMEM((8, plan.late, block_rows, LANES), BF16),
            pltpu.VMEM((late_rows, LANES), F32),
            pltpu.VMEM((width, width), BF16),
            pltpu.VMEM((width, hidden), BF16),
            pltpu.VMEM((hidden, width), BF16),
            pltpu.VMEM((m, width), F32),
            pltpu.VMEM((m, width), F32),
            pltpu.SemaphoreType.DMA((8,)),
        ],
        name="mlp",
        flops=12 * m * width * hidden,
        moved=4 * late_rows * LANES,
    )
    grad_input, keep_early, send_early = call(
        functools.partial(back_kernel, plan),
        [x, in_one, qkv, mixed, lse, w_qkv, vecs, grad_mid, grad_mixed, tail],
        [vmem()] * 10,
        [
            ((slots, length, width), F32),
            ((4, plan.early, plan.shard, LANES), F32),
            ((4, plan.early, plan.shard, LANES), BF16),
        ],
        [
            pltpu.VMEM((plan.split, LANES), F32),
            pltpu.VMEM((m, 3 * width), BF16),
        ],
        name="back",
        flops=4 * m * width * 3 * width,
        moved=4 * plan.split * LANES,
    )
    late_sum = plane_sum(plan, keep_late, send_late)
    early_sum = plane_sum(plan, keep_early, send_early)
    half = plan.groups // 2
    acc, sent = call(
        functools.partial(join_kernel, plan),
        [*early_sum, *late_sum],
        [vmem()] * 4,
        [((half, plan.shard, LANES), F32), ((half, plan.shard, LANES), BF16)],
        name="join",
    )
    bit = 8
    while True:
        acc = acc + lax.ppermute(sent, "dp", bit_pairs(n, bit)).astype(F32)
        bit *= 2
        if bit == n:
            break
        acc = acc.reshape((-1, 2) + acc.shape[1:])
        acc, sent = acc[:, 0], acc[:, 1].astype(BF16)
    grad_params = acc.reshape(1, plan.shard * LANES) / total[0, 0]
    return act, grad_input, grad_params


def solution(mesh):
    n = mesh.shape["dp"]

    def step(images, params, counts, grad_out):
        plan = Plan(n, images.shape[2], FF, params.shape[1] * n, images.shape[1])
        return body(plan, images, params, counts, grad_out)

    placed = (P("dp", None, None), P(None, "dp"), P("dp"), P("dp", None, None))
    return jax.shard_map(
        step,
        mesh=mesh,
        in_specs=placed,
        out_specs=(P("dp", None, None), P("dp", None, None), P(None, "dp")),
        check_vma=False,
    )
```

```python
import functools

import jax
import jax.numpy as jnp
from jax import lax
from jax.experimental import pallas as pl
from jax.experimental.pallas import tpu as pltpu
from jax.sharding import PartitionSpec as P

HEADS = 6
FF = 1536
EPS = 1e-06
LANES = 128
F32 = jnp.float32
BF16 = jnp.bfloat16
MIB = 1024 * 1024


class Plan:
    def __init__(self, n, width, hidden, flat, length):
        self.n = n
        self.width, self.hidden = width, hidden
        self.w, self.f = width // LANES, hidden // LANES
        self.length = length
        self.tokens = -(-length // 16) * 16
        self.shard = flat // n // LANES
        self.groups = n // 8
        self.early = self.groups // 4
        self.late = self.groups - self.early
        self.minor = max(16, (self.shard + 32) // 64 * 16)
        self.major = self.shard - self.minor
        w, f = self.w, self.f
        sizes = [
            ("gain_one", w),
            ("bias_one", w),
            ("w_qkv", width * 3 * w),
            ("q_bias", w),
            ("v_bias", w),
            ("w_out", width * w),
            ("out_bias", w),
            ("gain_two", w),
            ("bias_two", w),
            ("w_up", width * f),
            ("up_bias", f),
            ("w_down", hidden * w),
            ("down_bias", w),
        ]
        self.at = {}
        row = 0
        for name, count in sizes:
            self.at[name] = row
            row += count
        self.used = row
        self.rows = flat // LANES
        self.split = self.early * 8 * self.shard
        self.base = self.at["w_out"] // 8 * 8
        self.tail = self.split - self.base
        assert self.base <= self.at["w_out"] <= self.split


def lane_mask(rows):
    return lax.broadcasted_iota(jnp.int32, (rows, LANES), 1) < LANES // 2


def load_vec(ref, row, count):
    return jnp.concatenate([ref[row + i : row + i + 1, :] for i in range(count)], axis=1)


def load_mat(ref, row, rows, count, out):
    for c in range(count):
        out[:, c * LANES : (c + 1) * LANES] = ref[pl.ds(row + c, rows, stride=count), :].astype(BF16)


def store_vec(ref, row, count, value):
    for i in range(count):
        ref[row + i : row + i + 1, :] = value[:, i * LANES : (i + 1) * LANES]


def store_mat(ref, row, rows, count, value, first=0):
    for c in range(value.shape[1] // LANES):
        ref[pl.ds(row + first + c, rows, stride=count), :] = value[:, c * LANES : (c + 1) * LANES]


def dot(left, right):
    return lax.dot_general(left, right, (((1,), (0,)), ((), ())), preferred_element_type=F32)


def dot_nt(left, right):
    return lax.dot_general(left, right, (((1,), (1,)), ((), ())), preferred_element_type=F32)


def dot_tn(left, right):
    return lax.dot_general(left, right, (((0,), (0,)), ((), ())), preferred_element_type=F32)


def norm(stream):
    mean = jnp.mean(stream, axis=-1, keepdims=True)
    centred = stream - mean
    variance = jnp.mean(centred * centred, axis=-1, keepdims=True)
    inv_std = lax.rsqrt(variance + EPS)
    return centred * inv_std, inv_std


def norm_back(grad, normed, inv_std, gain):
    grad_gain = jnp.sum(grad * normed, axis=0, keepdims=True)
    grad_bias = jnp.sum(grad, axis=0, keepdims=True)
    scaled = grad * gain
    grad_in = inv_std * (
        scaled
        - jnp.mean(scaled, axis=-1, keepdims=True)
        - normed * jnp.mean(scaled * normed, axis=-1, keepdims=True)
    )
    return grad_in, grad_gain, grad_bias


def axis_bits(core):
    return 2 + 2 * core, 4 - 2 * core


def piece_owner(me, piece):
    low = me % 8
    core = low % 2
    if piece & 4:
        low = low ^ 1
        core = 1 - core
    first, second = axis_bits(core)
    if piece & 1:
        low = low ^ first
    if piece & 2:
        low = low ^ second
    return low


def mixed_pairs(n, flip):
    return [(i, i ^ axis_bits(i % 2)[flip]) for i in range(n)]


def bit_pairs(n, bit):
    return [(i, i ^ bit) for i in range(n)]


def unpack_rows(plan, majors, minors, flat, first, groups, origin, cnt):
    me = lax.axis_index("dp")
    mine = me // 8
    for p, piece in enumerate(majors):
        low = piece_owner(me, p)
        for t in range(first, first + groups):
            row = (8 * t + low) * plan.shard - origin
            flat[pl.ds(row, plan.major), :] = piece[mine ^ t].astype(F32)
    for i, piece in enumerate(minors):
        t = mine ^ (i % plan.groups)

        @pl.when(jnp.logical_and(t >= first, t < first + groups))
        def _(i=i, piece=piece, t=t):
            for place in range(4):
                low = piece_owner(me, place + 4 * (i // plan.groups))
                row = (8 * t + low) * plan.shard + plan.major - origin
                block = piece[place].astype(F32)
                flat[pl.ds(row, plan.minor), :] = block[: plan.minor]
                cnt[...] += block[plan.minor : plan.minor + 1]


def pack_rows(plan, flat, first, groups, origin, outs):
    me = lax.axis_index("dp")
    for far in (0, 1):
        low_ref, high_ref, minor_ref = outs[3 * far : 3 * far + 3]
        for place in range(4):
            low = piece_owner(me, place + 4 * far)
            major_ref = low_ref if place < 2 else high_ref
            for t in range(groups):
                row = (8 * (first + t) + low) * plan.shard - origin
                at = place % 2 * groups + t
                major_ref[at] = flat[pl.ds(row, plan.major), :].astype(major_ref.dtype)
                at = place * groups + t
                minor_ref[at] = flat[pl.ds(row + plan.major, plan.minor), :].astype(minor_ref.dtype)


def packed_shapes(plan, groups):
    return [
        (shape, kind)
        for kind in (F32, BF16)
        for shape in (
            (2 * groups, plan.major, LANES),
            (2 * groups, plan.major, LANES),
            (4 * groups, plan.minor, LANES),
        )
    ]


def prepare_kernel(plan, counts, images, grads, x_out, grad_out, normed_out, inv_out):
    tokens, length = plan.tokens, plan.length
    for b in range(images.shape[0]):
        rows = slice(b * tokens, b * tokens + length)
        rest = slice(b * tokens + length, (b + 1) * tokens)
        live = (counts[0] > b).astype(F32)
        x = images[b]
        x_out[rows, :] = x
        grad_out[rows, :] = (grads[b].astype(F32) * live).astype(BF16)
        normed, inv_std = norm(x.astype(F32))
        normed_out[rows, :] = normed
        inv_out[rows, :] = inv_std
        for ref in (x_out, grad_out, normed_out, inv_out):
            ref[rest, :] = jnp.zeros((tokens - length, ref.shape[1]), ref.dtype)


def attend_kernel(plan, normed_ref, *refs):
    majors, refs = refs[:8], refs[8:]
    minors, refs = refs[: 2 * plan.groups], refs[2 * plan.groups :]
    in_one, qkv, mixed, lse, w_qkv, vecs, tail, cnt_ref, flat = refs
    at, w, width = plan.at, plan.w, plan.width
    tokens = plan.tokens
    cnt_ref[...] = jnp.zeros((1, LANES), F32)
    unpack_rows(plan, majors, minors, flat, 0, plan.early, 0, cnt_ref)
    tail[...] = flat[plan.base : plan.split, :]
    load_mat(flat, at["w_qkv"], width, 3 * w, w_qkv)
    gain = load_vec(flat, at["gain_one"], w)
    bias = load_vec(flat, at["bias_one"], w)
    vecs[0:1, :] = gain
    shifted = (normed_ref[...] * gain + bias).astype(BF16)
    in_one[...] = shifted
    biases = [load_vec(flat, at["q_bias"], w), None, load_vec(flat, at["v_bias"], w)]
    for third in range(3):
        cols = slice(third * width, (third + 1) * width)
        project = dot(shifted, w_qkv[:, cols])
        if biases[third] is not None:
            project = project + biases[third]
        qkv[:, cols] = project.astype(BF16)
    scale = (width // HEADS) ** (-0.5)
    mask = lane_mask(tokens)
    valid = lax.broadcasted_iota(jnp.int32, (2 * tokens, tokens), 1) < plan.length
    zero = jnp.zeros((tokens, LANES), BF16)
    for b in range(normed_ref.shape[0] // tokens):
        rows = slice(b * tokens, (b + 1) * tokens)
        for p in range(w):
            q = qkv[rows, p * LANES : (p + 1) * LANES]
            k = qkv[rows, width + p * LANES : width + (p + 1) * LANES]
            v = qkv[rows, 2 * width + p * LANES : 2 * width + (p + 1) * LANES]
            q2 = jnp.concatenate([jnp.where(mask, q, zero), jnp.where(mask, zero, q)], axis=0)
            scores = jnp.where(valid, dot_nt(q2, k) * scale, -1e30)
            peak = jnp.max(scores, axis=-1, keepdims=True)
            exps = jnp.exp(scores - peak)
            total = jnp.sum(exps, axis=-1, keepdims=True)
            lse[b * w + p] = peak + jnp.log(total)
            weights = (exps * (1.0 / total)).astype(BF16)
            out = dot(weights, v)
            mixed[rows, p * LANES : (p + 1) * LANES] = jnp.where(
                mask, out[:tokens], out[tokens:]
            ).astype(BF16)


def mlp_kernel(plan, chunk, counts, x_ref, grad_ref, mixed_ref, tail_ref, cnt_ref, *refs):
    majors, refs = refs[:8], refs[8:]
    minors, refs = refs[: 2 * plan.groups], refs[2 * plan.groups :]
    act, grad_mid, grad_mixed, tail, total = refs[:5]
    packed = refs[5:11]
    flat, w_out, w_up, w_down, acc, grad_in = refs[11:]
    at, w, f, width = plan.at, plan.w, plan.f, plan.width
    tokens, base = plan.tokens, plan.base
    slots = x_ref.shape[0] // tokens
    flat[0 : plan.tail, :] = tail_ref[...]
    total[...] = cnt_ref[...]
    unpack_rows(plan, majors, minors, flat, plan.early, plan.late, base, total)
    load_mat(flat, at["w_out"] - base, width, w, w_out)
    load_mat(flat, at["w_up"] - base, width, f, w_up)
    load_mat(flat, at["w_down"] - base, plan.hidden, w, w_down)
    vec = lambda name, count: load_vec(flat, at[name] - base, count)
    out_bias, gain, bias = vec("out_bias", w), vec("gain_two", w), vec("bias_two", w)
    up_bias, down_bias = vec("up_bias", f), vec("down_bias", w)

    row = lax.broadcasted_iota(jnp.int32, (slots * tokens, 1), 0)
    live = (row < counts[0] * tokens).astype(F32)
    grad_low = grad_ref[...]
    grad = grad_low.astype(F32)
    mixed = mixed_ref[...]
    middle = x_ref[...].astype(F32) + dot(mixed, w_out[...]) + out_bias
    normed, inv_std = norm(middle)
    in_two = (normed * gain + bias).astype(BF16)
    in_two_t = in_two.T
    store_vec(flat, at["down_bias"] - base, w, jnp.sum(grad, axis=0, keepdims=True))
    for c in range(plan.hidden // chunk):
        cols = slice(c * chunk, (c + 1) * chunk)
        pre = dot(in_two, w_up[:, cols]) + up_bias[:, cols]
        phi = 0.5 * (1.0 + lax.erf(pre * 0.7071067811865476))
        slope = phi + pre * jnp.exp(-0.5 * pre * pre) * 0.3989422804014327
        hidden = (pre * phi).astype(BF16)
        grad_pre = dot_nt(grad_low, w_down[cols, :]) * slope
        pre_low = grad_pre.astype(BF16)
        out = dot(hidden, w_down[cols, :])
        back = dot_nt(pre_low, w_up[:, cols])
        if c == 0:
            acc[...] = out
            grad_in[...] = back
        else:
            acc[...] += out
            grad_in[...] += back
        store_mat(
            flat, at["w_down"] - base + c * chunk * w, chunk, w, dot_tn(hidden, grad_low)
        )
        store_mat(
            flat, at["w_up"] - base, width, f, dot(in_two_t, pre_low), c * chunk // LANES
        )
        store_vec(
            flat,
            at["up_bias"] - base + c * chunk // LANES,
            chunk // LANES,
            jnp.sum(grad_pre, axis=0, keepdims=True),
        )
    result = ((middle + acc[...] + down_bias) * live).astype(BF16)
    for b in range(slots):
        act[b] = result[b * tokens : b * tokens + plan.length]
    norm_grad, grad_gain, grad_bias = norm_back(grad_in[...], normed, inv_std, gain)
    mid = grad + norm_grad
    grad_mid[...] = mid
    mid_low = mid.astype(BF16)
    store_vec(flat, at["gain_two"] - base, w, grad_gain)
    store_vec(flat, at["bias_two"] - base, w, grad_bias)
    store_vec(flat, at["out_bias"] - base, w, jnp.sum(mid, axis=0, keepdims=True))
    store_mat(flat, at["w_out"] - base, width, w, dot_tn(mixed, mid_low))
    grad_mixed[...] = dot_nt(mid_low, w_out[...]).astype(BF16)
    if plan.rows > plan.used:
        flat[plan.used - base :, :] = jnp.zeros((plan.rows - plan.used, LANES), F32)
    tail[...] = flat[0 : plan.tail, :]
    pack_rows(plan, flat, plan.early, plan.late, base, packed)


def attend_back_kernel(plan, qkv, mixed_ref, lse, grad_mixed, proj, sums):
    w, width = plan.w, plan.width
    tokens = plan.tokens
    slots = qkv.shape[0] // tokens
    scale = (width // HEADS) ** (-0.5)
    mask = lane_mask(tokens)
    valid = lax.broadcasted_iota(jnp.int32, (2 * tokens, tokens), 1) < plan.length
    zero = jnp.zeros((tokens, LANES), BF16)
    both = lambda v: jnp.concatenate([jnp.where(mask, v, zero), jnp.where(mask, zero, v)], axis=0)
    for p in range(w):
        cut = slice(p * LANES, (p + 1) * LANES)
        k_cut = slice(width + p * LANES, width + (p + 1) * LANES)
        v_cut = slice(2 * width + p * LANES, 2 * width + (p + 1) * LANES)
        q_sum = jnp.zeros((1, LANES), F32)
        v_sum = jnp.zeros((1, LANES), F32)
        for b in range(slots):
            rows = slice(b * tokens, (b + 1) * tokens)
            k, v = qkv[rows, k_cut], qkv[rows, v_cut]
            q2 = both(qkv[rows, cut])
            g2 = both(grad_mixed[rows, cut])
            m = mixed_ref[rows, cut].astype(F32)
            scores = dot_nt(q2, k) * scale
            probs = jnp.where(valid, jnp.exp(scores - lse[b * w + p]), 0.0)
            grad_values = dot_tn(probs.astype(BF16), g2)
            grad_weights = dot_nt(g2, v)
            row_dot = jnp.sum(
                g2.astype(F32) * jnp.concatenate([m, m], axis=0), axis=-1, keepdims=True
            )
            grad_scores = (probs * (grad_weights - row_dot) * scale).astype(BF16)
            pair = dot(grad_scores, k)
            grad_queries = jnp.where(mask, pair[:tokens], pair[tokens:])
            grad_keys = dot_tn(grad_scores, q2)
            q_sum = q_sum + jnp.sum(grad_queries, axis=0, keepdims=True)
            v_sum = v_sum + jnp.sum(grad_values, axis=0, keepdims=True)
            proj[rows, cut] = grad_queries.astype(BF16)
            proj[rows, k_cut] = grad_keys.astype(BF16)
            proj[rows, v_cut] = grad_values.astype(BF16)
        sums[p : p + 1, :] = q_sum
        sums[w + p : w + p + 1, :] = v_sum


def project_back_kernel(
    plan, in_one, proj, sums, w_qkv, vecs, grad_mid, normed_ref, inv_ref, tail, *refs
):
    grad_input, packed, flat = refs[0], refs[1:7], refs[7]
    at, w, width = plan.at, plan.w, plan.width
    tokens = plan.tokens
    flat[plan.base : plan.split, :] = tail[...]
    flat[at["q_bias"] : at["q_bias"] + w, :] = sums[0:w, :]
    flat[at["v_bias"] : at["v_bias"] + w, :] = sums[w : 2 * w, :]
    in_one_t = in_one[...].T
    for third in range(3):
        cols = slice(third * width, (third + 1) * width)
        store_mat(flat, at["w_qkv"], width, 3 * w, dot(in_one_t, proj[:, cols]), third * w)
    grad_in = dot_nt(proj[...], w_qkv[...])
    norm_grad, grad_gain, grad_bias = norm_back(
        grad_in, normed_ref[...], inv_ref[...], vecs[0:1, :]
    )
    store_vec(flat, at["gain_one"], w, grad_gain)
    store_vec(flat, at["bias_one"], w, grad_bias)
    result = grad_mid[...] + norm_grad
    for b in range(grad_input.shape[0]):
        grad_input[b] = result[b * tokens : b * tokens + plan.length]
    pack_rows(plan, flat, 0, plan.early, 0, packed)


def join_kernel(plan, places, early, early_in, late, late_in, keep, *sends):
    mine = lax.axis_index("dp") // 8
    for r in range(plan.groups):
        t = mine ^ r
        out = keep if r == 0 else sends[r - 1]
        for place in range(places):

            @pl.when(t < plan.early)
            def _(out=out, place=place, t=t):
                at = place * plan.early + t
                out[place] = (early[at] + early_in[at].astype(F32)).astype(out.dtype)

            @pl.when(t >= plan.early)
            def _(out=out, place=place, t=t):
                at = place * plan.late + t - plan.early
                out[place] = (late[at] + late_in[at].astype(F32)).astype(out.dtype)


def vmem():
    return pl.BlockSpec(memory_space=pltpu.VMEM)


def call(kernel, ins, outs, scratch=(), flops=0, moved=0, limit=24, specs=None):
    return pl.pallas_call(
        kernel,
        in_specs=specs or [vmem()] * len(ins),
        out_specs=tuple(vmem() for _ in outs),
        out_shape=tuple(jax.ShapeDtypeStruct(s, d) for s, d in outs),
        scratch_shapes=list(scratch),
        compiler_params=pltpu.CompilerParams(vmem_limit_bytes=limit * MIB),
        cost_estimate=pl.CostEstimate(flops=flops, bytes_accessed=moved, transcendentals=0),
    )(*ins)


def hop(plan, piece, flip):
    return lax.ppermute(piece, "dp", mixed_pairs(plan.n, flip))


def across(plan, piece):
    return lax.ppermute(piece, "dp", bit_pairs(plan.n, 1))


def between(plan, piece, rel):
    return lax.ppermute(piece, "dp", bit_pairs(plan.n, 8 * rel))


def gather(plan, block, prepared):
    rels = range(1, plan.groups)
    major, minor = block[:, : plan.major], block[:, plan.major :]
    column = [major] + [between(plan, major, r) for r in rels]
    plane = [minor, hop(plan, minor, 0), hop(plan, minor, 1)]
    plane = plane + [hop(plan, plane[1], 1)]
    column, plane, prepared = lax.optimization_barrier((column, plane, prepared))
    column, plane = jnp.concatenate(column, axis=0), jnp.concatenate(plane, axis=0)
    majors = [column, hop(plan, column, 0), hop(plan, column, 1)]
    majors = majors + [hop(plan, majors[1], 1)]
    minors = [plane] + [between(plan, plane, r) for r in rels]
    majors = majors + [across(plan, p) for p in majors]
    minors = minors + [across(plan, p) for p in minors]
    return majors, minors, prepared


def plane_sum(plan, keep_low, keep_high, came_low, came_high, blocks):
    came = hop(plan, (keep_high + came_high.astype(F32)).astype(BF16), 1).astype(F32)
    low = keep_low + came_low.astype(F32)
    last = hop(plan, (low[blocks:] + came[blocks:]).astype(BF16), 0)
    return low[:blocks] + came[:blocks], last


def join(plan, places, rows, parts):
    shape = (places, rows, LANES)
    return call(
        functools.partial(join_kernel, plan, places),
        parts,
        [(shape, F32)] + [(shape, BF16)] * (plan.groups - 1),
        limit=8,
        moved=12 * plan.groups * places * rows * LANES,
    )


def scatter_sum(plan, early, late):
    rels = range(1, plan.groups)
    e_low, e_high, e_minor, e_low_in, e_high_in, e_minor_in = early
    l_low, l_high, l_minor, l_low_in, l_high_in, l_minor_in = late
    early_sum = plane_sum(plan, e_low, e_high, e_low_in, e_high_in, plan.early)
    late_sum = plane_sum(plan, l_low, l_high, l_low_in, l_high_in, plan.late)
    minor, *sends = join(plan, 4, plan.minor, [e_minor, e_minor_in, l_minor, l_minor_in])
    for r in rels:
        minor = minor + between(plan, sends[r - 1], r).astype(F32)
    minor = minor[:2] + hop(plan, minor[2:].astype(BF16), 1).astype(F32)
    minor = minor[:1] + hop(plan, minor[1:].astype(BF16), 0).astype(F32)
    major, *sends = join(plan, 1, plan.major, [*early_sum, *late_sum])
    for r in rels:
        major = major + between(plan, sends[r - 1], r).astype(F32)
    return jnp.concatenate([major, minor], axis=1)


def exchange(plan, packed):
    low, high, minor, low_out, high_out, minor_out = packed
    high_in = across(plan, high_out)
    low_in = across(plan, low_out)
    minor_in = across(plan, minor_out)
    return low, high, minor, low_in, high_in, minor_in


def body(plan, images, params, counts, grad_out):
    slots, length, width = images.shape
    tokens = plan.tokens
    m = slots * tokens
    w, hidden = plan.w, plan.hidden
    late_rows = plan.rows - plan.base
    smem = pl.BlockSpec(memory_space=pltpu.SMEM)

    count_row = jnp.broadcast_to(counts.astype(BF16)[:, None, None], (1, 1, LANES))
    block = jnp.concatenate([params.reshape(1, plan.shard, LANES), count_row], axis=1)
    prepared = call(
        functools.partial(prepare_kernel, plan),
        [counts, images, grad_out],
        [((m, width), BF16), ((m, width), BF16), ((m, width), F32), ((m, 1), F32)],
        specs=[smem, vmem(), vmem()],
        flops=20 * m * width,
        moved=12 * m * width,
        limit=8,
    )
    majors, minors, (x, grad, normed, inv_std) = gather(plan, block, prepared)
    in_one, qkv, mixed, lse, w_qkv, vecs, tail, cnt = call(
        functools.partial(attend_kernel, plan),
        [normed] + majors + minors,
        [
            ((m, width), BF16),
            ((m, 3 * width), BF16),
            ((m, width), BF16),
            ((slots * w, 2 * tokens, 1), F32),
            ((width, 3 * width), BF16),
            ((8, width), F32),
            ((plan.tail, LANES), F32),
            ((1, LANES), F32),
        ],
        [pltpu.VMEM((plan.split, LANES), F32)],
        flops=2 * m * width * 3 * width,
        moved=4 * plan.split * LANES,
        limit=16,
    )
    act, grad_mid, grad_mixed, tail, total, *late = call(
        functools.partial(mlp_kernel, plan, 2 * LANES),
        [counts, x, grad, mixed, tail, cnt] + majors + minors,
        [
            ((slots, length, width), BF16),
            ((m, width), F32),
            ((m, width), BF16),
            ((plan.tail, LANES), F32),
            ((1, LANES), F32),
        ]
        + packed_shapes(plan, plan.late),
        [
            pltpu.VMEM((late_rows, LANES), F32),
            pltpu.VMEM((width, width), BF16),
            pltpu.VMEM((width, hidden), BF16),
            pltpu.VMEM((hidden, width), BF16),
            pltpu.VMEM((m, width), F32),
            pltpu.VMEM((m, width), F32),
        ],
        specs=[smem] + [vmem()] * (13 + 2 * plan.groups),
        flops=12 * m * width * hidden,
        moved=4 * late_rows * LANES,
        limit=32,
    )
    late = exchange(plan, late)
    proj, sums = call(
        functools.partial(attend_back_kernel, plan),
        [qkv, mixed, lse, grad_mixed],
        [((m, 3 * width), BF16), ((-(-2 * w // 8) * 8, LANES), F32)],
        flops=20 * m * tokens * width,
        moved=8 * m * width,
        limit=12,
    )
    grad_input, *early = call(
        functools.partial(project_back_kernel, plan),
        [in_one, proj, sums, w_qkv, vecs, grad_mid, normed, inv_std, tail],
        [((slots, length, width), F32)] + packed_shapes(plan, plan.early),
        [pltpu.VMEM((plan.split, LANES), F32)],
        flops=4 * m * width * 3 * width,
        moved=4 * plan.split * LANES,
        limit=16,
    )
    acc = scatter_sum(plan, exchange(plan, early), late)
    grad_params = acc.reshape(1, plan.shard * LANES) / total[0, 0]
    return act, grad_input, grad_params


def solution(mesh):
    n = mesh.shape["dp"]

    def step(images, params, counts, grad_out):
        plan = Plan(n, images.shape[2], FF, params.shape[1] * n, images.shape[1])
        return body(plan, images, params, counts, grad_out)

    placed = (P("dp", None, None), P(None, "dp"), P("dp"), P("dp", None, None))
    return jax.shard_map(
        step,
        mesh=mesh,
        in_specs=placed,
        out_specs=(P("dp", None, None), P("dp", None, None), P(None, "dp")),
        check_vma=False,
    )
```

```python
import functools

import jax
import jax.numpy as jnp
from jax import lax
from jax.experimental import pallas as pl
from jax.experimental.pallas import tpu as pltpu
from jax.sharding import PartitionSpec as P

HEADS = 6
FF = 1536
EPS = 1e-06
LANES = 128
F32 = jnp.float32
BF16 = jnp.bfloat16
MIB = 1024 * 1024


class Plan:
    def __init__(self, n, width, hidden, flat, length):
        self.n = n
        self.width, self.hidden = width, hidden
        self.w, self.f = width // LANES, hidden // LANES
        self.length = length
        self.tokens = -(-length // 16) * 16
        self.shard = flat // n // LANES
        self.groups = n // 8
        self.early = self.groups // 4
        self.late = self.groups - self.early
        self.minor = max(16, self.shard * 22 // 64 // 16 * 16)
        self.major = self.shard - self.minor
        self.sum_minor = max(16, self.shard * 15 // 64 // 16 * 16)
        self.sum_major = self.shard - self.sum_minor
        w, f = self.w, self.f
        sizes = [
            ("gain_one", w),
            ("bias_one", w),
            ("w_qkv", width * 3 * w),
            ("q_bias", w),
            ("v_bias", w),
            ("w_out", width * w),
            ("out_bias", w),
            ("gain_two", w),
            ("bias_two", w),
            ("w_up", width * f),
            ("up_bias", f),
            ("w_down", hidden * w),
            ("down_bias", w),
        ]
        self.at = {}
        row = 0
        for name, count in sizes:
            self.at[name] = row
            row += count
        self.used = row
        self.rows = flat // LANES
        self.split = self.early * 8 * self.shard
        self.base = self.at["w_out"] // 8 * 8
        self.tail = self.split - self.base
        assert self.base <= self.at["w_out"] <= self.split


def lane_mask(rows):
    return lax.broadcasted_iota(jnp.int32, (rows, LANES), 1) < LANES // 2


def load_vec(ref, row, count):
    return jnp.concatenate([ref[row + i : row + i + 1, :] for i in range(count)], axis=1)


def load_mat(ref, row, rows, count, out):
    for c in range(count):
        out[:, c * LANES : (c + 1) * LANES] = ref[pl.ds(row + c, rows, stride=count), :].astype(BF16)


def store_vec(ref, row, count, value):
    for i in range(count):
        ref[row + i : row + i + 1, :] = value[:, i * LANES : (i + 1) * LANES]


def store_mat(ref, row, rows, count, value, first=0):
    for c in range(value.shape[1] // LANES):
        ref[pl.ds(row + first + c, rows, stride=count), :] = value[:, c * LANES : (c + 1) * LANES]


def dot(left, right):
    return lax.dot_general(left, right, (((1,), (0,)), ((), ())), preferred_element_type=F32)


def dot_nt(left, right):
    return lax.dot_general(left, right, (((1,), (1,)), ((), ())), preferred_element_type=F32)


def dot_tn(left, right):
    return lax.dot_general(left, right, (((0,), (0,)), ((), ())), preferred_element_type=F32)


def norm(stream):
    mean = jnp.mean(stream, axis=-1, keepdims=True)
    centred = stream - mean
    variance = jnp.mean(centred * centred, axis=-1, keepdims=True)
    inv_std = lax.rsqrt(variance + EPS)
    return centred * inv_std, inv_std


def norm_back(grad, normed, inv_std, gain):
    grad_gain = jnp.sum(grad * normed, axis=0, keepdims=True)
    grad_bias = jnp.sum(grad, axis=0, keepdims=True)
    scaled = grad * gain
    grad_in = inv_std * (
        scaled
        - jnp.mean(scaled, axis=-1, keepdims=True)
        - normed * jnp.mean(scaled * normed, axis=-1, keepdims=True)
    )
    return grad_in, grad_gain, grad_bias


def axis_bits(core):
    return 2 + 2 * core, 4 - 2 * core


def piece_owner(me, piece):
    low = me % 8
    core = low % 2
    if piece & 4:
        low = low ^ 1
        core = 1 - core
    first, second = axis_bits(core)
    if piece & 1:
        low = low ^ first
    if piece & 2:
        low = low ^ second
    return low


def mixed_pairs(n, flip):
    return [(i, i ^ axis_bits(i % 2)[flip]) for i in range(n)]


def bit_pairs(n, bit):
    return [(i, i ^ bit) for i in range(n)]


def unpack_rows(plan, majors, minors, flat, first, groups, origin, cnt):
    me = lax.axis_index("dp")
    mine = me // 8
    for p, piece in enumerate(majors):
        low = piece_owner(me, p)
        for t in range(first, first + groups):
            row = (8 * t + low) * plan.shard - origin
            flat[pl.ds(row, plan.major), :] = piece[mine ^ t].astype(F32)
    for i, piece in enumerate(minors):
        t = mine ^ (i % plan.groups)

        @pl.when(jnp.logical_and(t >= first, t < first + groups))
        def _(i=i, piece=piece, t=t):
            for place in range(4):
                low = piece_owner(me, place + 4 * (i // plan.groups))
                row = (8 * t + low) * plan.shard + plan.major - origin
                block = piece[place].astype(F32)
                flat[pl.ds(row, plan.minor), :] = block[: plan.minor]
                cnt[...] += block[plan.minor : plan.minor + 1]


def pack_rows(plan, flat, first, groups, origin, outs):
    me = lax.axis_index("dp")
    for far in (0, 1):
        low_ref, high_ref, minor_ref = outs[3 * far : 3 * far + 3]
        for place in range(4):
            low = piece_owner(me, place + 4 * far)
            major_ref = low_ref if place < 2 else high_ref
            for t in range(groups):
                row = (8 * (first + t) + low) * plan.shard - origin
                at = place % 2 * groups + t
                major_ref[at] = flat[pl.ds(row, plan.sum_major), :].astype(major_ref.dtype)
                at = place * groups + t
                minor_ref[at] = flat[pl.ds(row + plan.sum_major, plan.sum_minor), :].astype(minor_ref.dtype)


def packed_shapes(plan, groups):
    return [
        (shape, kind)
        for kind in (F32, BF16)
        for shape in (
            (2 * groups, plan.sum_major, LANES),
            (2 * groups, plan.sum_major, LANES),
            (4 * groups, plan.sum_minor, LANES),
        )
    ]


def prepare_kernel(plan, counts, images, grads, x_out, grad_out, normed_out, inv_out):
    tokens, length = plan.tokens, plan.length
    for b in range(images.shape[0]):
        rows = slice(b * tokens, b * tokens + length)
        rest = slice(b * tokens + length, (b + 1) * tokens)
        live = (counts[0] > b).astype(F32)
        x = images[b]
        x_out[rows, :] = x
        grad_out[rows, :] = (grads[b].astype(F32) * live).astype(BF16)
        normed, inv_std = norm(x.astype(F32))
        normed_out[rows, :] = normed
        inv_out[rows, :] = inv_std
        for ref in (x_out, grad_out, normed_out, inv_out):
            ref[rest, :] = jnp.zeros((tokens - length, ref.shape[1]), ref.dtype)


def attend_kernel(plan, normed_ref, *refs):
    majors, refs = refs[:8], refs[8:]
    minors, refs = refs[: 2 * plan.groups], refs[2 * plan.groups :]
    in_one, qkv, mixed, lse, w_qkv, vecs, tail, cnt_ref, flat = refs
    at, w, width = plan.at, plan.w, plan.width
    tokens = plan.tokens
    cnt_ref[...] = jnp.zeros((1, LANES), F32)
    unpack_rows(plan, majors, minors, flat, 0, plan.early, 0, cnt_ref)
    tail[...] = flat[plan.base : plan.split, :]
    load_mat(flat, at["w_qkv"], width, 3 * w, w_qkv)
    gain = load_vec(flat, at["gain_one"], w)
    bias = load_vec(flat, at["bias_one"], w)
    vecs[0:1, :] = gain
    shifted = (normed_ref[...] * gain + bias).astype(BF16)
    in_one[...] = shifted
    biases = [load_vec(flat, at["q_bias"], w), None, load_vec(flat, at["v_bias"], w)]
    for third in range(3):
        cols = slice(third * width, (third + 1) * width)
        project = dot(shifted, w_qkv[:, cols])
        if biases[third] is not None:
            project = project + biases[third]
        qkv[:, cols] = project.astype(BF16)
    scale = (width // HEADS) ** (-0.5)
    mask = lane_mask(tokens)
    valid = lax.broadcasted_iota(jnp.int32, (2 * tokens, tokens), 1) < plan.length
    zero = jnp.zeros((tokens, LANES), BF16)
    for b in range(normed_ref.shape[0] // tokens):
        rows = slice(b * tokens, (b + 1) * tokens)
        for p in range(w):
            q = qkv[rows, p * LANES : (p + 1) * LANES]
            k = qkv[rows, width + p * LANES : width + (p + 1) * LANES]
            v = qkv[rows, 2 * width + p * LANES : 2 * width + (p + 1) * LANES]
            q2 = jnp.concatenate([jnp.where(mask, q, zero), jnp.where(mask, zero, q)], axis=0)
            scores = jnp.where(valid, dot_nt(q2, k) * scale, -1e30)
            peak = jnp.max(scores, axis=-1, keepdims=True)
            exps = jnp.exp(scores - peak)
            total = jnp.sum(exps, axis=-1, keepdims=True)
            lse[b * w + p] = peak + jnp.log(total)
            weights = (exps * (1.0 / total)).astype(BF16)
            out = dot(weights, v)
            mixed[rows, p * LANES : (p + 1) * LANES] = jnp.where(
                mask, out[:tokens], out[tokens:]
            ).astype(BF16)


def mlp_kernel(plan, chunk, counts, x_ref, grad_ref, mixed_ref, tail_ref, cnt_ref, *refs):
    majors, refs = refs[:8], refs[8:]
    minors, refs = refs[: 2 * plan.groups], refs[2 * plan.groups :]
    act, grad_mid, grad_mixed, tail, total = refs[:5]
    packed = refs[5:11]
    flat, w_out, w_up, w_down, acc, grad_in = refs[11:]
    at, w, f, width = plan.at, plan.w, plan.f, plan.width
    tokens, base = plan.tokens, plan.base
    slots = x_ref.shape[0] // tokens
    flat[0 : plan.tail, :] = tail_ref[...]
    total[...] = cnt_ref[...]
    unpack_rows(plan, majors, minors, flat, plan.early, plan.late, base, total)
    load_mat(flat, at["w_out"] - base, width, w, w_out)
    load_mat(flat, at["w_up"] - base, width, f, w_up)
    load_mat(flat, at["w_down"] - base, plan.hidden, w, w_down)
    vec = lambda name, count: load_vec(flat, at[name] - base, count)
    out_bias, gain, bias = vec("out_bias", w), vec("gain_two", w), vec("bias_two", w)
    up_bias, down_bias = vec("up_bias", f), vec("down_bias", w)

    row = lax.broadcasted_iota(jnp.int32, (slots * tokens, 1), 0)
    live = (row < counts[0] * tokens).astype(F32)
    grad_low = grad_ref[...]
    grad = grad_low.astype(F32)
    mixed = mixed_ref[...]
    middle = x_ref[...].astype(F32) + dot(mixed, w_out[...]) + out_bias
    normed, inv_std = norm(middle)
    in_two = (normed * gain + bias).astype(BF16)
    in_two_t = in_two.T
    store_vec(flat, at["down_bias"] - base, w, jnp.sum(grad, axis=0, keepdims=True))
    for c in range(plan.hidden // chunk):
        cols = slice(c * chunk, (c + 1) * chunk)
        pre = dot(in_two, w_up[:, cols]) + up_bias[:, cols]
        phi = 0.5 * (1.0 + lax.erf(pre * 0.7071067811865476))
        slope = phi + pre * jnp.exp(-0.5 * pre * pre) * 0.3989422804014327
        hidden = (pre * phi).astype(BF16)
        grad_pre = dot_nt(grad_low, w_down[cols, :]) * slope
        pre_low = grad_pre.astype(BF16)
        out = dot(hidden, w_down[cols, :])
        back = dot_nt(pre_low, w_up[:, cols])
        if c == 0:
            acc[...] = out
            grad_in[...] = back
        else:
            acc[...] += out
            grad_in[...] += back
        store_mat(
            flat, at["w_down"] - base + c * chunk * w, chunk, w, dot_tn(hidden, grad_low)
        )
        store_mat(
            flat, at["w_up"] - base, width, f, dot(in_two_t, pre_low), c * chunk // LANES
        )
        store_vec(
            flat,
            at["up_bias"] - base + c * chunk // LANES,
            chunk // LANES,
            jnp.sum(grad_pre, axis=0, keepdims=True),
        )
    result = ((middle + acc[...] + down_bias) * live).astype(BF16)
    for b in range(slots):
        act[b] = result[b * tokens : b * tokens + plan.length]
    norm_grad, grad_gain, grad_bias = norm_back(grad_in[...], normed, inv_std, gain)
    mid = grad + norm_grad
    grad_mid[...] = mid
    mid_low = mid.astype(BF16)
    store_vec(flat, at["gain_two"] - base, w, grad_gain)
    store_vec(flat, at["bias_two"] - base, w, grad_bias)
    store_vec(flat, at["out_bias"] - base, w, jnp.sum(mid, axis=0, keepdims=True))
    store_mat(flat, at["w_out"] - base, width, w, dot_tn(mixed, mid_low))
    grad_mixed[...] = dot_nt(mid_low, w_out[...]).astype(BF16)
    if plan.rows > plan.used:
        flat[plan.used - base :, :] = jnp.zeros((plan.rows - plan.used, LANES), F32)
    tail[...] = flat[0 : plan.tail, :]
    pack_rows(plan, flat, plan.early, plan.late, base, packed)


def attend_back_kernel(plan, qkv, mixed_ref, lse, grad_mixed, proj, sums):
    w, width = plan.w, plan.width
    tokens = plan.tokens
    slots = qkv.shape[0] // tokens
    scale = (width // HEADS) ** (-0.5)
    mask = lane_mask(tokens)
    valid = lax.broadcasted_iota(jnp.int32, (2 * tokens, tokens), 1) < plan.length
    zero = jnp.zeros((tokens, LANES), BF16)
    both = lambda v: jnp.concatenate([jnp.where(mask, v, zero), jnp.where(mask, zero, v)], axis=0)
    for p in range(w):
        cut = slice(p * LANES, (p + 1) * LANES)
        k_cut = slice(width + p * LANES, width + (p + 1) * LANES)
        v_cut = slice(2 * width + p * LANES, 2 * width + (p + 1) * LANES)
        q_sum = jnp.zeros((1, LANES), F32)
        v_sum = jnp.zeros((1, LANES), F32)
        for b in range(slots):
            rows = slice(b * tokens, (b + 1) * tokens)
            k, v = qkv[rows, k_cut], qkv[rows, v_cut]
            q2 = both(qkv[rows, cut])
            g2 = both(grad_mixed[rows, cut])
            m = mixed_ref[rows, cut].astype(F32)
            scores = dot_nt(q2, k) * scale
            probs = jnp.where(valid, jnp.exp(scores - lse[b * w + p]), 0.0)
            grad_values = dot_tn(probs.astype(BF16), g2)
            grad_weights = dot_nt(g2, v)
            row_dot = jnp.sum(
                g2.astype(F32) * jnp.concatenate([m, m], axis=0), axis=-1, keepdims=True
            )
            grad_scores = (probs * (grad_weights - row_dot) * scale).astype(BF16)
            pair = dot(grad_scores, k)
            grad_queries = jnp.where(mask, pair[:tokens], pair[tokens:])
            grad_keys = dot_tn(grad_scores, q2)
            q_sum = q_sum + jnp.sum(grad_queries, axis=0, keepdims=True)
            v_sum = v_sum + jnp.sum(grad_values, axis=0, keepdims=True)
            proj[rows, cut] = grad_queries.astype(BF16)
            proj[rows, k_cut] = grad_keys.astype(BF16)
            proj[rows, v_cut] = grad_values.astype(BF16)
        sums[p : p + 1, :] = q_sum
        sums[w + p : w + p + 1, :] = v_sum


def project_back_kernel(
    plan, in_one, proj, sums, w_qkv, vecs, grad_mid, normed_ref, inv_ref, tail, *refs
):
    grad_input, packed, flat = refs[0], refs[1:7], refs[7]
    at, w, width = plan.at, plan.w, plan.width
    tokens = plan.tokens
    flat[plan.base : plan.split, :] = tail[...]
    flat[at["q_bias"] : at["q_bias"] + w, :] = sums[0:w, :]
    flat[at["v_bias"] : at["v_bias"] + w, :] = sums[w : 2 * w, :]
    in_one_t = in_one[...].T
    for third in range(3):
        cols = slice(third * width, (third + 1) * width)
        store_mat(flat, at["w_qkv"], width, 3 * w, dot(in_one_t, proj[:, cols]), third * w)
    grad_in = dot_nt(proj[...], w_qkv[...])
    norm_grad, grad_gain, grad_bias = norm_back(
        grad_in, normed_ref[...], inv_ref[...], vecs[0:1, :]
    )
    store_vec(flat, at["gain_one"], w, grad_gain)
    store_vec(flat, at["bias_one"], w, grad_bias)
    result = grad_mid[...] + norm_grad
    for b in range(grad_input.shape[0]):
        grad_input[b] = result[b * tokens : b * tokens + plan.length]
    pack_rows(plan, flat, 0, plan.early, 0, packed)


def join_kernel(plan, places, early, early_in, late, late_in, keep, *sends):
    mine = lax.axis_index("dp") // 8
    for r in range(plan.groups):
        t = mine ^ r
        out = keep if r == 0 else sends[r - 1]
        for place in range(places):

            @pl.when(t < plan.early)
            def _(out=out, place=place, t=t):
                at = place * plan.early + t
                out[place] = (early[at] + early_in[at].astype(F32)).astype(out.dtype)

            @pl.when(t >= plan.early)
            def _(out=out, place=place, t=t):
                at = place * plan.late + t - plan.early
                out[place] = (late[at] + late_in[at].astype(F32)).astype(out.dtype)


def vmem():
    return pl.BlockSpec(memory_space=pltpu.VMEM)


def call(kernel, ins, outs, scratch=(), flops=0, moved=0, limit=24, specs=None):
    return pl.pallas_call(
        kernel,
        in_specs=specs or [vmem()] * len(ins),
        out_specs=tuple(vmem() for _ in outs),
        out_shape=tuple(jax.ShapeDtypeStruct(s, d) for s, d in outs),
        scratch_shapes=list(scratch),
        compiler_params=pltpu.CompilerParams(vmem_limit_bytes=limit * MIB),
        cost_estimate=pl.CostEstimate(flops=flops, bytes_accessed=moved, transcendentals=0),
    )(*ins)


def hop(plan, piece, flip):
    return lax.ppermute(piece, "dp", mixed_pairs(plan.n, flip))


def across(plan, piece):
    return lax.ppermute(piece, "dp", bit_pairs(plan.n, 1))


def between(plan, piece, rel):
    return lax.ppermute(piece, "dp", bit_pairs(plan.n, 8 * rel))


def gather(plan, block, prepared):
    rels = range(1, plan.groups)
    major, minor = block[:, : plan.major], block[:, plan.major :]
    column = [major] + [between(plan, major, r) for r in rels]
    plane = [minor, hop(plan, minor, 0), hop(plan, minor, 1)]
    plane = plane + [hop(plan, plane[1], 1)]
    column, plane = lax.optimization_barrier((column, plane))
    column, plane = jnp.concatenate(column, axis=0), jnp.concatenate(plane, axis=0)
    majors = [column, hop(plan, column, 0), hop(plan, column, 1)]
    majors[1], prepared = lax.optimization_barrier((majors[1], prepared))
    majors = majors + [hop(plan, majors[1], 1)]
    minors = [plane] + [between(plan, plane, r) for r in rels]
    majors = majors + [across(plan, p) for p in majors]
    minors = minors + [across(plan, p) for p in minors]
    return majors, minors, prepared


def plane_sum(plan, keep_low, keep_high, came_low, came_high, blocks):
    came = hop(plan, (keep_high + came_high.astype(F32)).astype(BF16), 1).astype(F32)
    low = keep_low + came_low.astype(F32)
    high = (low[blocks:] + came[blocks:]).astype(BF16)
    last = hop(plan, high, 0)
    return low[:blocks] + came[:blocks], last


def join(plan, places, rows, parts):
    shape = (places, rows, LANES)
    return call(
        functools.partial(join_kernel, plan, places),
        parts,
        [(shape, F32)] + [(shape, BF16)] * (plan.groups - 1),
        limit=8,
        moved=12 * plan.groups * places * rows * LANES,
    )


def scatter_sum(plan, early, late):
    rels = range(1, plan.groups)
    e_low, e_high, e_minor, e_low_in, e_high_in, e_minor_in = early
    l_low, l_high, l_minor, l_low_in, l_high_in, l_minor_in = late
    early_sum = plane_sum(plan, e_low, e_high, e_low_in, e_high_in, plan.early)
    late_sum = plane_sum(plan, l_low, l_high, l_low_in, l_high_in, plan.late)
    minor, *sends = join(plan, 4, plan.sum_minor, [e_minor, e_minor_in, l_minor, l_minor_in])
    for r in rels:
        minor = minor + between(plan, sends[r - 1], r).astype(F32)
    minor = minor[:2] + hop(plan, minor[2:].astype(BF16), 1).astype(F32)
    minor = minor[:1] + hop(plan, minor[1:].astype(BF16), 0).astype(F32)
    major, *sends = join(plan, 1, plan.sum_major, [*early_sum, *late_sum])
    for r in rels:
        major = major + between(plan, sends[r - 1], r).astype(F32)
    return jnp.concatenate([major, minor], axis=1)


def exchange(plan, packed):
    low, high, minor, low_out, high_out, minor_out = packed
    high_in = across(plan, high_out)
    low_in = across(plan, low_out)
    minor_in = across(plan, minor_out)
    return low, high, minor, low_in, high_in, minor_in


def body(plan, images, params, counts, grad_out):
    slots, length, width = images.shape
    tokens = plan.tokens
    m = slots * tokens
    w, hidden = plan.w, plan.hidden
    late_rows = plan.rows - plan.base
    smem = pl.BlockSpec(memory_space=pltpu.SMEM)

    count_row = jnp.broadcast_to(counts.astype(BF16)[:, None, None], (1, 1, LANES))
    block = jnp.concatenate([params.reshape(1, plan.shard, LANES), count_row], axis=1)
    prepared = call(
        functools.partial(prepare_kernel, plan),
        [counts, images, grad_out],
        [((m, width), BF16), ((m, width), BF16), ((m, width), F32), ((m, 1), F32)],
        specs=[smem, vmem(), vmem()],
        flops=20 * m * width,
        moved=12 * m * width,
        limit=8,
    )
    majors, minors, (x, grad, normed, inv_std) = gather(plan, block, prepared)
    in_one, qkv, mixed, lse, w_qkv, vecs, tail, cnt = call(
        functools.partial(attend_kernel, plan),
        [normed] + majors + minors,
        [
            ((m, width), BF16),
            ((m, 3 * width), BF16),
            ((m, width), BF16),
            ((slots * w, 2 * tokens, 1), F32),
            ((width, 3 * width), BF16),
            ((8, width), F32),
            ((plan.tail, LANES), F32),
            ((1, LANES), F32),
        ],
        [pltpu.VMEM((plan.split, LANES), F32)],
        flops=2 * m * width * 3 * width,
        moved=4 * plan.split * LANES,
        limit=16,
    )
    act, grad_mid, grad_mixed, tail, total, *late = call(
        functools.partial(mlp_kernel, plan, 4 * LANES),
        [counts, x, grad, mixed, tail, cnt] + majors + minors,
        [
            ((slots, length, width), BF16),
            ((m, width), F32),
            ((m, width), BF16),
            ((plan.tail, LANES), F32),
            ((1, LANES), F32),
        ]
        + packed_shapes(plan, plan.late),
        [
            pltpu.VMEM((late_rows, LANES), F32),
            pltpu.VMEM((width, width), BF16),
            pltpu.VMEM((width, hidden), BF16),
            pltpu.VMEM((hidden, width), BF16),
            pltpu.VMEM((m, width), F32),
            pltpu.VMEM((m, width), F32),
        ],
        specs=[smem] + [vmem()] * (13 + 2 * plan.groups),
        flops=12 * m * width * hidden,
        moved=4 * late_rows * LANES,
        limit=32,
    )
    late = exchange(plan, late)
    proj, sums = call(
        functools.partial(attend_back_kernel, plan),
        [qkv, mixed, lse, grad_mixed],
        [((m, 3 * width), BF16), ((-(-2 * w // 8) * 8, LANES), F32)],
        flops=20 * m * tokens * width,
        moved=8 * m * width,
        limit=12,
    )
    grad_input, *early = call(
        functools.partial(project_back_kernel, plan),
        [in_one, proj, sums, w_qkv, vecs, grad_mid, normed, inv_std, tail],
        [((slots, length, width), F32)] + packed_shapes(plan, plan.early),
        [pltpu.VMEM((plan.split, LANES), F32)],
        flops=4 * m * width * 3 * width,
        moved=4 * plan.split * LANES,
        limit=16,
    )
    acc = scatter_sum(plan, exchange(plan, early), late)
    grad_params = acc.reshape(1, plan.shard * LANES) / total[0, 0]
    return act, grad_input, grad_params


def solution(mesh):
    n = mesh.shape["dp"]

    def step(images, params, counts, grad_out):
        plan = Plan(n, images.shape[2], FF, params.shape[1] * n, images.shape[1])
        return body(plan, images, params, counts, grad_out)

    placed = (P("dp", None, None), P(None, "dp"), P("dp"), P("dp", None, None))
    return jax.shard_map(
        step,
        mesh=mesh,
        in_specs=placed,
        out_specs=(P("dp", None, None), P("dp", None, None), P(None, "dp")),
        check_vma=False,
    )
```
